512 devices in a mesh: row: 8 (over z_lo), col: 16 (over x, y), depth: 4 (over z_hi, core).
Axes of the slice: x: 4, y: 4, z: 16 (z_hi: 2, z_lo: 8; z = z_hi * 8 + z_lo), core: 2. Of those that a mesh axis runs over, the one named last changes fastest.
Arguments:
- tokens: bfloat16 [512, 12288], P(('col', 'depth'), 'row'), may hold values from -6 to 6
- cotangent: bfloat16 [512, 12288], P(('col', 'depth'), 'row'), may hold values from -0.375 to 0.375
- w_in: bfloat16 [12288, 24576], P('row', ('col', 'depth')), may hold values from -0.0546875 to 0.0546875
- b_in: float32 [24576], P('col'), may hold values from -4 to 4
- w_out: bfloat16 [24576, 12288], P('col', ('row', 'depth')), may hold values from -0.0390625 to 0.0390625
Outputs:
- input_grad: bfloat16 [512, 12288], P(('col', 'depth'), 'row')
- w_in_grad: bfloat16 [12288, 24576], P('row', ('col', 'depth'))
- b_in_grad: float32 [24576], P(('col', 'depth'))
- w_out_grad: bfloat16 [24576, 12288], P('col', ('row', 'depth'))
The draws below stay inside these ranges and needn't reach their ends.
All inputs are finite; a program needn't handle non-finite values.
Results may differ from the reference program's by a relative error of at most 0.0065.
Values may be sent and summed in bfloat16 or wider, within the bound.
No kernel may reach another device: no remote copies, remote signals or barrier semaphores. Data moves between devices by JAX's collectives and lax.ppermute only.
A program may use at most 64 MiB of HBM per device.

```python
import jax
import jax.numpy as jnp

D = 12288
H = 24576
TOKENS = 512


def levels(key, extent, cuts, low, largest):
    def one(axis_at, blocks):
        steps = jax.random.uniform(jax.random.fold_in(jax.random.fold_in(key, 6), axis_at), (blocks,), jnp.float32, low / len(cuts), largest / len(cuts))
        return jnp.repeat(jnp.exp(steps), extent[axis_at] // blocks).reshape((-1,) + (1,) * (len(extent) - axis_at - 1))

    gain = one(*cuts[0])
    for cut in cuts[1:]:
        gain = gain * one(*cut)
    return gain


def normal_values(own_key, extent, deviation, limit, split=(), dtype=jnp.bfloat16):
    loudness = levels(own_key, extent, split, -0.22, 0.18) if split else 1.0
    values = jax.random.normal(own_key, extent, jnp.float32) * deviation * loudness
    return jnp.minimum(jnp.maximum(values, -limit), limit).astype(dtype)


def setup_inputs(seed: int = 0) -> dict:
    streams_of = jax.random.split(jax.random.key(seed), 6)
    tokens = normal_values(streams_of[0], (TOKENS, D), 1.0, 6.0, ((0, 64), (1, 8)))
    cotangent = normal_values(streams_of[1], (TOKENS, D), 0.0625, 0.375, ((0, 64), (1, 8)))
    w_in = normal_values(streams_of[2], (D, H), D ** -0.5, 0.0546875, ((0, 8), (1, 64)))
    b_in = normal_values(streams_of[3], (H,), 1.0, 4.0, ((0, 16),), jnp.float32)
    w_out = normal_values(streams_of[4], (H, D), H ** -0.5, 0.0390625, ((0, 16), (1, 32)))
    return {"tokens": tokens, "cotangent": cotangent, "w_in": w_in, "b_in": b_in, "w_out": w_out}


coef = 0.7978845608


def gelu_pair(pre):
    inner = coef * (pre + 0.044715 * pre * pre * pre)
    tanh_v = jnp.tanh(inner)
    act = 0.5 * pre * (1.0 + tanh_v)
    slope = 0.5 * (1.0 + tanh_v) + 0.5 * pre * (1.0 - tanh_v * tanh_v) * coef * (1.0 + 0.134145 * pre * pre)
    return act, slope


def reference(tokens, cotangent, w_in, b_in, w_out):
    pre = jnp.dot(tokens, w_in, preferred_element_type=jnp.float32) + b_in
    act_f, slope = gelu_pair(pre)
    act = act_f.astype(jnp.bfloat16)
    back = jnp.dot(cotangent, w_out.T, preferred_element_type=jnp.float32)
    grad_pre = (back * slope).astype(jnp.bfloat16)
    w_out_grad = jnp.dot(act.T, cotangent, preferred_element_type=jnp.float32).astype(jnp.bfloat16)
    w_in_grad = jnp.dot(tokens.T, grad_pre, preferred_element_type=jnp.float32).astype(jnp.bfloat16)
    b_in_grad = jnp.sum(grad_pre.astype(jnp.float32), axis=0)
    input_grad = jnp.dot(grad_pre, w_in.T, preferred_element_type=jnp.float32).astype(jnp.bfloat16)
    return input_grad, w_in_grad, b_in_grad, w_out_grad
```

```python
import jax
import jax.numpy as jnp
from jax import lax
from jax.sharding import Mesh, PartitionSpec as P

coef = 0.7978845608
bf16 = jnp.bfloat16
f32 = jnp.float32
SWAP = [(0, 1), (1, 0)]
GRID = ("x", "y")


def gelu_pair(pre):
    inner = coef * (pre + 0.044715 * pre * pre * pre)
    tanh_v = jnp.tanh(inner)
    act = 0.5 * pre * (1.0 + tanh_v)
    slope = 0.5 * (1.0 + tanh_v) + 0.5 * pre * (1.0 - tanh_v * tanh_v) * coef * (
        1.0 + 0.134145 * pre * pre
    )
    return (act, slope)


def dot(left, right):
    return jnp.dot(left, right, preferred_element_type=f32)


def against(left, right):
    return lax.dot_general(left, right, (((1,), (1,)), ((), ())), preferred_element_type=f32)


def over_rows(left, right):
    return lax.dot_general(left, right, (((0,), (0,)), ((), ())), preferred_element_type=f32)


def part_of(whole, at, size, dim):
    return lax.dynamic_slice_in_dim(whole, at * size, size, dim)


def swap(value, axis):
    return lax.ppermute(value, axis, SWAP)


def join(mine, other, axis, dim):
    first = lax.axis_index(axis) == 0
    return jnp.where(
        first,
        jnp.concatenate([mine, other], dim),
        jnp.concatenate([other, mine], dim),
    )


def widen(mine, axis, dim):
    return join(mine, swap(mine, axis), axis, dim)


def halve(part, axis, dim=0):
    size = part.shape[dim] // 2
    at = lax.axis_index(axis)
    out = part_of(part, 1 - at, size, dim).astype(bf16)
    return part_of(part, at, size, dim) + swap(out, axis).astype(f32)


def spread(rows):
    n = lax.axis_size("x") * lax.axis_size("y")
    sent = jnp.broadcast_to(rows[None], (n,) + rows.shape)
    got = lax.all_to_all(sent, GRID, 0, 0, tiled=True)
    return got.reshape(n * rows.shape[0], rows.shape[1])


def shards(tokens, cotangent, w_in, b_in, w_out):
    zh = lax.axis_index("zh")
    core = lax.axis_index("core")
    feat = tokens.shape[1]
    quarter = w_in.shape[1]
    half_h = 2 * quarter
    half_d = 2 * w_out.shape[1]

    in_pair = lax.all_gather(w_in, "core", axis=1, tiled=True)
    out_pair = lax.all_gather(w_out, "core", axis=1, tiled=True)

    sent = jnp.concatenate([tokens, part_of(cotangent, 1 - zh, half_d, 1)], 1)
    kept = jnp.concatenate([tokens, part_of(cotangent, zh, half_d, 1)], 1)
    both = join(kept, swap(sent, "zh"), "zh", 0)
    every_g = spread(both[:, feat:])
    every_x = spread(both[:, :feat])

    back = against(every_g, out_pair)
    pre = dot(every_x, in_pair)
    for axis in ("rl", "rm", "rh"):
        back = halve(back, axis)
        pre = halve(pre, axis)
    back = halve(back, "zh", 1)

    act_f, slope = gelu_pair(pre + part_of(b_in, zh, half_h, 0))
    act = act_f.astype(bf16)
    grad = (back * slope).astype(bf16)

    for axis in ("rh", "rm", "rl"):
        grad = widen(grad, axis, 0)

    part = against(grad, in_pair).astype(bf16)
    n = lax.axis_size("x") * lax.axis_size("y")
    got = lax.all_to_all(part.reshape(n, -1, feat), GRID, 0, 0, tiled=True)
    summed = jnp.sum(got.astype(f32), axis=0)
    input_grad = halve(summed, "zh").astype(bf16)

    pair_x = swap(every_x, "core")
    own_grad = part_of(grad, core, quarter, 1)
    pair_grad = swap(part_of(grad, 1 - core, quarter, 1), "core")
    w_in_grad = (over_rows(every_x, own_grad) + over_rows(pair_x, pair_grad)).astype(bf16)
    b_in_grad = jnp.sum(own_grad.astype(f32), 0) + jnp.sum(pair_grad.astype(f32), 0)

    act = widen(act, "zh", 1)
    for axis in ("rh", "rm", "rl"):
        act = widen(act, axis, 0)
    pair_act = swap(act, "core")
    own_g = part_of(every_g, core, w_out.shape[1], 1)
    pair_g = swap(part_of(every_g, 1 - core, w_out.shape[1], 1), "core")
    w_out_grad = (over_rows(act, own_g) + over_rows(pair_act, pair_g)).astype(bf16)
    return (input_grad, w_in_grad, b_in_grad, w_out_grad)


def solution(mesh):
    grid = Mesh(
        mesh.devices.reshape(2, 2, 2, 4, 4, 2, 2), ("rh", "rm", "rl", "x", "y", "zh", "core")
    )
    row, col, depth = ("rh", "rm", "rl"), ("x", "y"), ("zh", "core")
    return jax.shard_map(
        shards,
        mesh=grid,
        in_specs=(
            P(col + depth, row),
            P(col + depth, row),
            P(row, col + depth),
            P(col),
            P(col, row + depth),
        ),
        out_specs=(
            P(col + depth, row),
            P(row, col + depth),
            P(col + depth),
            P(col, row + depth),
        ),
        check_vma=False,
    )
```

```python
import jax
import jax.numpy as jnp
from jax import lax
from jax.sharding import Mesh, PartitionSpec as P

coef = 0.7978845608
bf16 = jnp.bfloat16
f32 = jnp.float32
SWAP = [(0, 1), (1, 0)]
GRID = ("x", "y")
ROW4 = ("rm", "rl")


def gelu_pair(pre):
    inner = coef * (pre + 0.044715 * pre * pre * pre)
    tanh_v = jnp.tanh(inner)
    act = 0.5 * pre * (1.0 + tanh_v)
    slope = 0.5 * (1.0 + tanh_v) + 0.5 * pre * (1.0 - tanh_v * tanh_v) * coef * (
        1.0 + 0.134145 * pre * pre
    )
    return (act, slope)


def dot(left, right):
    return jnp.dot(left, right, preferred_element_type=f32)


def against(left, right):
    return lax.dot_general(left, right, (((1,), (1,)), ((), ())), preferred_element_type=f32)


def over_rows(left, right):
    return lax.dot_general(left, right, (((0,), (0,)), ((), ())), preferred_element_type=f32)


def part_of(whole, at, size, dim):
    return lax.dynamic_slice_in_dim(whole, at * size, size, dim)


def swap(value, axis):
    return lax.ppermute(value, axis, SWAP)


def join(mine, other, axis, dim):
    first = lax.axis_index(axis) == 0
    return jnp.where(
        first,
        jnp.concatenate([mine, other], dim),
        jnp.concatenate([other, mine], dim),
    )


def widen(mine, axis, dim):
    return join(mine, swap(mine, axis), axis, dim)


def cut(part, axis, dim=0):
    size = part.shape[dim] // 2
    at = lax.axis_index(axis)
    return part_of(part, at, size, dim), part_of(part, 1 - at, size, dim).astype(bf16)


def halve(part, axis, dim=0):
    kept, sent = cut(part, axis, dim)
    return kept + swap(sent, axis).astype(f32)


def spread(rows, axes):
    n = lax.axis_size(axes)
    sent = jnp.broadcast_to(rows[None], (n,) + rows.shape)
    got = lax.all_to_all(sent, axes, 0, 0, tiled=True)
    return got.reshape(n * rows.shape[0], rows.shape[1])


def deal(part, axes):
    n = lax.axis_size(axes)
    return lax.all_to_all(part.reshape(n, -1, part.shape[1]), axes, 0, 0, tiled=True)


def total(parts):
    return jnp.sum(parts.astype(f32), axis=0)


def flip(value, axis):
    size = value.shape[1] // 2
    other = jnp.concatenate([value[:, size:], value[:, :size]], 1)
    return jnp.where(lax.axis_index(axis) == 0, value, other)


def shards(tokens, cotangent, w_in, b_in, w_out):
    zh = lax.axis_index("zh")
    feat = tokens.shape[1]
    quarter = w_in.shape[1]
    half_h = 2 * quarter
    quarter_d = w_out.shape[1]
    half_d = 2 * quarter_d

    sent = jnp.concatenate([tokens, part_of(cotangent, 1 - zh, half_d, 1)], 1)
    kept = jnp.concatenate([tokens, part_of(cotangent, zh, half_d, 1)], 1)
    got = swap(sent, "zh")
    w_out, w_in, got = lax.optimization_barrier((w_out, w_in, got))
    pair_out = swap(w_out, "core")
    pair_in = swap(w_in, "core")
    both = join(kept, got, "zh", 0)

    every_g = spread(flip(both[:, feat:], "core"), GRID)
    own_g, other_g = every_g[:, :quarter_d], every_g[:, quarter_d:]
    back = against(own_g, w_out) + against(other_g, pair_out)
    back = back.reshape(2, 2, -1, back.shape[1])
    back_kept, back_sent = cut(back, "rl", 1)
    back_sent, x_rows = lax.optimization_barrier((back_sent, both[:, :feat]))
    back_got = swap(back_sent, "rl")
    every_x = spread(x_rows, GRID)
    back_kept, back_sent = cut(back_kept + back_got.astype(f32), "rm", 0)
    back_sent, every_x = lax.optimization_barrier((back_sent, every_x))
    back_got = swap(back_sent, "rm")
    pre = jnp.concatenate([dot(every_x, w_in), dot(every_x, pair_in)], 1).astype(bf16)
    pre_parts = deal(pre, ROW4)
    back_kept, back_sent = cut((back_kept + back_got.astype(f32))[0, 0], "rh", 0)
    back_sent, pre_parts = lax.optimization_barrier((back_sent, pre_parts))
    back = back_kept + swap(back_sent, "rh").astype(f32)
    pre = halve(total(pre_parts), "rh")
    back = halve(back, "zh", 1)

    act_f, slope = gelu_pair(flip(pre, "core") + part_of(b_in, zh, half_h, 0))
    act = act_f.astype(bf16)
    grad = flip((back * slope).astype(bf16), "core")

    grad = spread(widen(grad, "rh", 0), ROW4)
    own_grad, other_grad = grad[:, :quarter], grad[:, quarter:]
    part = (against(own_grad, w_in) + against(other_grad, pair_in)).astype(bf16)
    act = widen(widen(act, "zh", 1), "rh", 0)[None, None]
    part, act = lax.optimization_barrier((part, act))
    input_grad = halve(total(deal(part, GRID)), "zh").astype(bf16)
    act = widen(widen(act, "rm", 0), "rl", 1).reshape(-1, act.shape[-1])

    pair_x = swap(every_x, "core")
    pair_grad = swap(other_grad, "core")
    w_in_grad = (over_rows(every_x, own_grad) + over_rows(pair_x, pair_grad)).astype(bf16)
    b_in_grad = jnp.sum(own_grad.astype(f32), 0) + jnp.sum(pair_grad.astype(f32), 0)

    pair_act = swap(act, "core")
    pair_g = swap(other_g, "core")
    w_out_grad = (over_rows(act, own_g) + over_rows(pair_act, pair_g)).astype(bf16)
    return (input_grad, w_in_grad, b_in_grad, w_out_grad)


def solution(mesh):
    grid = Mesh(
        mesh.devices.reshape(2, 2, 2, 4, 4, 2, 2), ("rh", "rm", "rl", "x", "y", "zh", "core")
    )
    row, col, depth = ("rh", "rm", "rl"), ("x", "y"), ("zh", "core")
    return jax.shard_map(
        shards,
        mesh=grid,
        in_specs=(
            P(col + depth, row),
            P(col + depth, row),
            P(row, col + depth),
            P(col),
            P(col, row + depth),
        ),
        out_specs=(
            P(col + depth, row),
            P(row, col + depth),
            P(col + depth),
            P(col, row + depth),
        ),
        check_vma=False,
    )
```

```python
import jax
import jax.numpy as jnp
from jax import lax
from jax.sharding import Mesh, PartitionSpec as P

coef = 0.7978845608
bf16 = jnp.bfloat16
f32 = jnp.float32
SWAP = [(0, 1), (1, 0)]
CROSS = [(0, 3), (1, 2), (2, 1), (3, 0)]
GRID = ("x", "y")
ROW4 = ("rm", "rl")


def gelu_pair(pre):
    inner = coef * (pre + 0.044715 * pre * pre * pre)
    tanh_v = jnp.tanh(inner)
    act = 0.5 * pre * (1.0 + tanh_v)
    slope = 0.5 * (1.0 + tanh_v) + 0.5 * pre * (1.0 - tanh_v * tanh_v) * coef * (
        1.0 + 0.134145 * pre * pre
    )
    return (act, slope)


def dot(left, right):
    return jnp.dot(left, right, preferred_element_type=f32)


def against(left, right):
    return lax.dot_general(left, right, (((1,), (1,)), ((), ())), preferred_element_type=f32)


def over_rows(left, right):
    return lax.dot_general(left, right, (((0,), (0,)), ((), ())), preferred_element_type=f32)


def part_of(whole, at, size, dim):
    return lax.dynamic_slice_in_dim(whole, at * size, size, dim)


def swap(value, axis):
    return lax.ppermute(value, axis, SWAP)


def join(mine, other, axis, dim):
    first = lax.axis_index(axis) == 0
    return jnp.where(
        first,
        jnp.concatenate([mine, other], dim),
        jnp.concatenate([other, mine], dim),
    )


def cross(value):
    return lax.ppermute(value, ("rh", "zh"), CROSS)


def both_sum(part, axis):
    part = part.astype(bf16)
    return part.astype(f32) + swap(part, axis).astype(f32)


def spread(rows, axes):
    n = lax.axis_size(axes)
    sent = jnp.broadcast_to(rows[None], (n,) + rows.shape)
    got = lax.all_to_all(sent, axes, 0, 0, tiled=True)
    return got.reshape(n * rows.shape[0], rows.shape[1])


def deal(part, axes):
    n = lax.axis_size(axes)
    got = lax.all_to_all(part.reshape(n, -1, part.shape[1]), axes, 0, 0, tiled=True)
    return jnp.sum(got.astype(f32), axis=0)


def shards(tokens, cotangent, w_in, b_in, w_out):
    zh = lax.axis_index("zh")
    core = lax.axis_index("core")
    tok_dev, feat = tokens.shape
    quarter = w_in.shape[1]
    half_h = 2 * quarter
    quarter_d = w_out.shape[1]
    half_d = 2 * quarter_d

    sent = jnp.concatenate([tokens, part_of(cotangent, 1 - zh, half_d, 1)], 1)
    kept = jnp.concatenate([tokens, part_of(cotangent, zh, half_d, 1)], 1)
    got = swap(sent, "zh")
    w_out, w_in, got = lax.optimization_barrier((w_out, w_in, got))
    out_pair = join(w_out, swap(w_out, "core"), "core", 1)
    in_pair = join(w_in, swap(w_in, "core"), "core", 1)

    every = spread(join(kept, got, "zh", 0), GRID)
    every_x, every_g = every[:, :feat], every[:, feat:]
    pre = dot(every_x, in_pair).astype(bf16)
    back = against(every_g, out_pair).astype(bf16)
    sums = deal(jnp.concatenate([pre, back], 1), ROW4)
    back = sums[:, half_h:]
    back_kept = part_of(back, zh, half_h, 1)
    back_sent = part_of(back, 1 - zh, half_h, 1).astype(bf16)
    pre = both_sum(sums[:, :half_h], "rh")
    back = both_sum(back_kept + cross(back_sent).astype(f32), "rh")

    act_f, slope = gelu_pair(pre + part_of(b_in, zh, half_h, 0))
    act = act_f.astype(bf16)
    act = join(act, cross(act), "zh", 1)
    grad = (back * slope).astype(bf16)
    gathered = spread(jnp.concatenate([grad, act], 1), ROW4)
    grad, act = gathered[:, :half_h], gathered[:, half_h:]

    part = against(grad, in_pair).astype(bf16)
    part, grad, act = lax.optimization_barrier((part, grad, act))
    summed = deal(part, GRID)
    out_rows = part_of(summed, 1 - zh, tok_dev, 0).astype(bf16)
    own_rows = part_of(summed, zh, tok_dev, 0)
    input_grad = (own_rows + swap(out_rows, "zh").astype(f32)).astype(bf16)

    pair_x = swap(every_x, "core")
    own_grad = part_of(grad, core, quarter, 1)
    pair_grad = swap(part_of(grad, 1 - core, quarter, 1), "core")
    w_in_grad = (over_rows(every_x, own_grad) + over_rows(pair_x, pair_grad)).astype(bf16)
    b_in_grad = jnp.sum(own_grad.astype(f32), 0) + jnp.sum(pair_grad.astype(f32), 0)

    own_g = part_of(every_g, core, quarter_d, 1)
    pair_g = swap(part_of(every_g, 1 - core, quarter_d, 1), "core")
    pair_act = swap(act, "core")
    w_out_grad = (over_rows(act, own_g) + over_rows(pair_act, pair_g)).astype(bf16)
    return (input_grad, w_in_grad, b_in_grad, w_out_grad)


def solution(mesh):
    grid = Mesh(
        mesh.devices.reshape(2, 2, 2, 4, 4, 2, 2), ("rh", "rm", "rl", "x", "y", "zh", "core")
    )
    row, col, depth = ("rh", "rm", "rl"), ("x", "y"), ("zh", "core")
    return jax.shard_map(
        shards,
        mesh=grid,
        in_specs=(
            P(col + depth, row),
            P(col + depth, row),
            P(row, col + depth),
            P(col),
            P(col, row + depth),
        ),
        out_specs=(
            P(col + depth, row),
            P(row, col + depth),
            P(col + depth),
            P(col, row + depth),
        ),
        check_vma=False,
    )
```

```python
import jax
import jax.numpy as jnp
from jax import lax
from jax.sharding import Mesh, PartitionSpec as P

coef = 0.7978845608
bf16 = jnp.bfloat16
f32 = jnp.float32
SWAP = [(0, 1), (1, 0)]
CROSS = [(0, 3), (1, 2), (2, 1), (3, 0)]
GRID = ("x", "y")
ROW4 = ("rm", "rl")


def gelu_pair(pre):
    inner = coef * (pre + 0.044715 * pre * pre * pre)
    tanh_v = jnp.tanh(inner)
    act = 0.5 * pre * (1.0 + tanh_v)
    slope = 0.5 * (1.0 + tanh_v) + 0.5 * pre * (1.0 - tanh_v * tanh_v) * coef * (
        1.0 + 0.134145 * pre * pre
    )
    return (act, slope)


def dot(left, right):
    return jnp.dot(left, right, preferred_element_type=f32)


def against(left, right):
    return lax.dot_general(left, right, (((1,), (1,)), ((), ())), preferred_element_type=f32)


def over_rows(left, right):
    return lax.dot_general(left, right, (((0,), (0,)), ((), ())), preferred_element_type=f32)


def part_of(whole, at, size, dim):
    return lax.dynamic_slice_in_dim(whole, at * size, size, dim)


def swap(value, axis):
    return lax.ppermute(value, axis, SWAP)


def join(mine, other, axis, dim):
    first = lax.axis_index(axis) == 0
    return jnp.where(
        first,
        jnp.concatenate([mine, other], dim),
        jnp.concatenate([other, mine], dim),
    )


def cut(part, axis, dim):
    size = part.shape[dim] // 2
    at = lax.axis_index(axis)
    return part_of(part, at, size, dim), part_of(part, 1 - at, size, dim).astype(bf16)


def cross(value):
    return lax.ppermute(value, ("rh", "zh"), CROSS)


def widen(mine, axis, dim):
    return join(mine, swap(mine, axis), axis, dim)


def spread(rows, axes):
    n = lax.axis_size(axes)
    sent = jnp.broadcast_to(rows[None], (n,) + rows.shape)
    got = lax.all_to_all(sent, axes, 0, 0, tiled=True)
    return got.reshape(n * rows.shape[0], rows.shape[1])


def deal(part, axes):
    n = lax.axis_size(axes)
    got = lax.all_to_all(part.reshape(n, -1, part.shape[1]), axes, 0, 0, tiled=True)
    if n > 4:
        return jnp.sum(got.astype(f32), axis=0)
    total = got[0].astype(f32)
    for at in range(1, n):
        total = total + got[at].astype(f32)
    return total


def shards(tokens, cotangent, w_in, b_in, w_out):
    zh = lax.axis_index("zh")
    core = lax.axis_index("core")
    tok_dev, feat = tokens.shape
    quarter = w_in.shape[1]
    half_h = 2 * quarter
    quarter_d = w_out.shape[1]
    half_d = 2 * quarter_d

    sent = jnp.concatenate([tokens, part_of(cotangent, 1 - zh, half_d, 1)], 1)
    kept = jnp.concatenate([tokens, part_of(cotangent, zh, half_d, 1)], 1)
    got = swap(sent, "zh")
    w_out, w_in, got = lax.optimization_barrier((w_out, w_in, got))
    out_pair = join(w_out, swap(w_out, "core"), "core", 1)
    in_pair = join(w_in, swap(w_in, "core"), "core", 1)

    rows = join(kept, got, "zh", 0)
    every_x = spread(rows[:, :feat], GRID)
    pre = dot(every_x, in_pair).reshape(2, 2, -1, half_h)
    pre_kept, pre_sent = cut(pre, "rl", 1)
    pre_sent, g_rows = lax.optimization_barrier((pre_sent, rows[:, feat:]))
    pre_kept, pre_sent = cut(pre_kept + swap(pre_sent, "rl").astype(f32), "rm", 0)
    every_g = spread(g_rows, GRID)
    pre_sent, every_g = lax.optimization_barrier((pre_sent, every_g))
    pre = (pre_kept + swap(pre_sent, "rm").astype(f32))[0, 0].astype(bf16)
    back = against(every_g, out_pair).astype(bf16)
    pre, back = lax.optimization_barrier((pre, back))
    sums = deal(back, ROW4).astype(bf16)
    pre = pre.astype(f32) + swap(pre, "rh").astype(f32)

    act_f, slope = gelu_pair(pre + part_of(b_in, zh, half_h, 0))
    act = act_f.astype(bf16)
    back_kept = part_of(sums, zh, half_h, 1)
    back_sent = part_of(sums, 1 - zh, half_h, 1)
    back_kept, back_sent, act = lax.optimization_barrier((back_kept, back_sent, act))
    near = back_kept.astype(f32) + swap(back_kept, "rh").astype(f32)
    far = cross(back_sent).astype(f32) + swap(back_sent, "zh").astype(f32)
    grad = ((near + far) * slope).astype(bf16)
    act = join(act, cross(act), "zh", 1)[None, None]

    grad = spread(grad, ROW4)
    part = against(grad, in_pair).astype(bf16)
    part, grad, act = lax.optimization_barrier((part, grad, act))
    summed = deal(part, GRID)
    act = widen(widen(act, "rm", 0), "rl", 1).reshape(-1, act.shape[-1])
    out_rows = part_of(summed, 1 - zh, tok_dev, 0).astype(bf16)
    own_rows = part_of(summed, zh, tok_dev, 0)
    input_grad = (own_rows + swap(out_rows, "zh").astype(f32)).astype(bf16)

    pair_x = swap(every_x, "core")
    own_grad = part_of(grad, core, quarter, 1)
    pair_grad = swap(part_of(grad, 1 - core, quarter, 1), "core")
    w_in_grad = (over_rows(every_x, own_grad) + over_rows(pair_x, pair_grad)).astype(bf16)
    b_in_grad = jnp.sum(own_grad.astype(f32), 0) + jnp.sum(pair_grad.astype(f32), 0)

    own_g = part_of(every_g, core, quarter_d, 1)
    pair_g = swap(part_of(every_g, 1 - core, quarter_d, 1), "core")
    pair_act = swap(act, "core")
    w_out_grad = (over_rows(act, own_g) + over_rows(pair_act, pair_g)).astype(bf16)
    return (input_grad, w_in_grad, b_in_grad, w_out_grad)


def solution(mesh):
    grid = Mesh(
        mesh.devices.reshape(2, 2, 2, 4, 4, 2, 2), ("rh", "rm", "rl", "x", "y", "zh", "core")
    )
    row, col, depth = ("rh", "rm", "rl"), ("x", "y"), ("zh", "core")
    return jax.shard_map(
        shards,
        mesh=grid,
        in_specs=(
            P(col + depth, row),
            P(col + depth, row),
            P(row, col + depth),
            P(col),
            P(col, row + depth),
        ),
        out_specs=(
            P(col + depth, row),
            P(row, col + depth),
            P(col + depth),
            P(col, row + depth),
        ),
        check_vma=False,
    )
```

```python
import jax
import jax.numpy as jnp
from jax import lax
from jax.sharding import Mesh, PartitionSpec as P

coef = 0.7978845608
bf16 = jnp.bfloat16
f32 = jnp.float32
SWAP = [(0, 1), (1, 0)]
CROSS = [(0, 3), (1, 2), (2, 1), (3, 0)]
GRID = ("x", "y")
ROW4 = ("rm", "rl")
RING4 = ("rh", "zh")


def gelu_pair(pre):
    inner = coef * (pre + 0.044715 * pre * pre * pre)
    tanh_v = jnp.tanh(inner)
    act = 0.5 * pre * (1.0 + tanh_v)
    slope = 0.5 * (1.0 + tanh_v) + 0.5 * pre * (1.0 - tanh_v * tanh_v) * coef * (
        1.0 + 0.134145 * pre * pre
    )
    return (act, slope)


def dot(left, right):
    return jnp.dot(left, right, preferred_element_type=f32)


def against(left, right):
    return lax.dot_general(left, right, (((1,), (1,)), ((), ())), preferred_element_type=f32)


def over_rows(left, right):
    return lax.dot_general(left, right, (((0,), (0,)), ((), ())), preferred_element_type=f32)


def part_of(whole, at, size, dim):
    return lax.dynamic_slice_in_dim(whole, at * size, size, dim)


def swap(value, axis):
    return lax.ppermute(value, axis, SWAP)


def join(mine, other, axis, dim):
    first = lax.axis_index(axis) == 0
    return jnp.where(
        first,
        jnp.concatenate([mine, other], dim),
        jnp.concatenate([other, mine], dim),
    )


def cut(part, axis, dim):
    size = part.shape[dim] // 2
    at = lax.axis_index(axis)
    return part_of(part, at, size, dim), part_of(part, 1 - at, size, dim).astype(bf16)


def cross(value):
    return lax.ppermute(value, ("rh", "zh"), CROSS)


def widen(mine, axis, dim):
    return join(mine, swap(mine, axis), axis, dim)


def spread(rows, axes):
    n = lax.axis_size(axes)
    sent = jnp.broadcast_to(rows[None], (n,) + rows.shape)
    got = lax.all_to_all(sent, axes, 0, 0, tiled=True)
    return got.reshape(n * rows.shape[0], rows.shape[1])


def deal(part, axes):
    n = lax.axis_size(axes)
    got = lax.all_to_all(part.reshape(n, -1, part.shape[1]), axes, 0, 0, tiled=True)
    if n > 4:
        return jnp.sum(got.astype(f32), axis=0)
    total = got[0].astype(f32)
    for at in range(1, n):
        total = total + got[at].astype(f32)
    return total


def shards(tokens, cotangent, w_in, b_in, w_out):
    zh = lax.axis_index("zh")
    core = lax.axis_index("core")
    tok_dev, feat = tokens.shape
    quarter = w_in.shape[1]
    half_h = 2 * quarter
    quarter_d = w_out.shape[1]
    half_d = 2 * quarter_d

    kept = jnp.concatenate([tokens, part_of(cotangent, zh, half_d, 1)], 1)
    sent = jnp.concatenate([tokens, part_of(cotangent, 1 - zh, half_d, 1)], 1)
    got = swap(sent, "zh")
    own = spread(kept, GRID)
    got, own, w_in, w_out = lax.optimization_barrier((got, own, w_in, w_out))
    in_pair = join(w_in, swap(w_in, "core"), "core", 1)
    out_pair = join(w_out, swap(w_out, "core"), "core", 1)
    other = spread(got, GRID)

    def by_token(mine, theirs):
        mine, theirs = (v.reshape(-1, tok_dev, v.shape[1]) for v in (mine, theirs))
        return join(mine, theirs, "zh", 1).reshape(-1, mine.shape[2])

    every = by_token(own, other)
    every_x, every_g = every[:, :feat], every[:, feat:]
    pre = dot(every_x, in_pair).astype(bf16)
    back = against(every_g, out_pair).astype(bf16)
    pre = deal(pre, ROW4).astype(bf16)
    pre, back = lax.optimization_barrier((pre, back))
    pre = pre.astype(f32) + swap(pre, "rh").astype(f32)
    sums = deal(back, ROW4).astype(bf16)

    act_f, slope = gelu_pair(pre + part_of(b_in, zh, half_h, 0))
    act = act_f.astype(bf16)
    crossed = cross(act)
    pair_x = swap(every_x, "core")
    pair_g = swap(part_of(every_g, 1 - core, quarter_d, 1), "core")
    sums, slope, crossed, pair_x, pair_g = lax.optimization_barrier(
        (sums, slope, crossed, pair_x, pair_g)
    )
    act = join(act, crossed, "zh", 1)[None, None]
    halves = jnp.stack([sums[:, :half_h], sums[:, half_h:]])
    halves = jnp.concatenate([halves, halves], 0).reshape(-1, half_h)
    grad = (deal(halves, RING4) * slope).astype(bf16)

    grad = spread(grad, ROW4)
    part = against(grad, in_pair).astype(bf16)
    part, grad, act = lax.optimization_barrier((part, grad, act))
    summed = deal(part, GRID)
    act = widen(act, "rm", 0)
    grad_sent, act = lax.optimization_barrier((part_of(grad, 1 - core, quarter, 1), act))
    act = widen(act, "rl", 1).reshape(-1, act.shape[-1])
    out_rows = part_of(summed, 1 - zh, tok_dev, 0).astype(bf16)
    own_rows = part_of(summed, zh, tok_dev, 0)
    input_grad = (own_rows + swap(out_rows, "zh").astype(f32)).astype(bf16)

    own_grad = part_of(grad, core, quarter, 1)
    pair_grad = swap(grad_sent, "core")
    w_in_grad = (over_rows(every_x, own_grad) + over_rows(pair_x, pair_grad)).astype(bf16)
    b_in_grad = jnp.sum(own_grad.astype(f32), 0) + jnp.sum(pair_grad.astype(f32), 0)

    own_g = part_of(every_g, core, quarter_d, 1)
    pair_act = swap(act, "core")
    w_out_grad = (over_rows(act, own_g) + over_rows(pair_act, pair_g)).astype(bf16)
    return (input_grad, w_in_grad, b_in_grad, w_out_grad)


def solution(mesh):
    grid = Mesh(
        mesh.devices.reshape(2, 2, 2, 4, 4, 2, 2), ("rh", "rm", "rl", "x", "y", "zh", "core")
    )
    row, col, depth = ("rh", "rm", "rl"), ("x", "y"), ("zh", "core")
    return jax.shard_map(
        shards,
        mesh=grid,
        in_specs=(
            P(col + depth, row),
            P(col + depth, row),
            P(row, col + depth),
            P(col),
            P(col, row + depth),
        ),
        out_specs=(
            P(col + depth, row),
            P(row, col + depth),
            P(col + depth),
            P(col, row + depth),
        ),
        check_vma=False,
    )
```

```python
import jax
import jax.numpy as jnp
from jax import lax
from jax.sharding import Mesh, PartitionSpec as P

coef = 0.7978845608
bf16 = jnp.bfloat16
f32 = jnp.float32
SWAP = [(0, 1), (1, 0)]
CROSS = [(0, 3), (1, 2), (2, 1), (3, 0)]
GRID = ("x", "y")
ROW4 = ("rm", "rl")


def gelu_pair(pre):
    inner = coef * (pre + 0.044715 * pre * pre * pre)
    tanh_v = jnp.tanh(inner)
    act = 0.5 * pre * (1.0 + tanh_v)
    slope = 0.5 * (1.0 + tanh_v) + 0.5 * pre * (1.0 - tanh_v * tanh_v) * coef * (
        1.0 + 0.134145 * pre * pre
    )
    return (act, slope)


def dot(left, right):
    return jnp.dot(left, right, preferred_element_type=f32)


def against(left, right):
    return lax.dot_general(left, right, (((1,), (1,)), ((), ())), preferred_element_type=f32)


def over_rows(left, right):
    return lax.dot_general(left, right, (((0,), (0,)), ((), ())), preferred_element_type=f32)


def part_of(whole, at, size, dim):
    return lax.dynamic_slice_in_dim(whole, at * size, size, dim)


def swap(value, axis):
    return lax.ppermute(value, axis, SWAP)


def join(mine, other, axis, dim):
    first = lax.axis_index(axis) == 0
    return jnp.where(
        first,
        jnp.concatenate([mine, other], dim),
        jnp.concatenate([other, mine], dim),
    )


def after(first, *values):
    kept = lax.optimization_barrier((first, *values))[1:]
    return kept[0] if len(kept) == 1 else kept


def cut(part, axis, dim):
    size = part.shape[dim] // 2
    at = lax.axis_index(axis)
    return part_of(part, at, size, dim), part_of(part, 1 - at, size, dim).astype(bf16)


def cross(value):
    return lax.ppermute(value, ("rh", "zh"), CROSS)


def widen(mine, axis, dim):
    return join(mine, swap(mine, axis), axis, dim)


def spread(rows, axes):
    n = lax.axis_size(axes)
    sent = jnp.broadcast_to(rows[None], (n,) + rows.shape)
    got = lax.all_to_all(sent, axes, 0, 0, tiled=True)
    return got.reshape(n * rows.shape[0], rows.shape[1])


def deal(part, axes):
    n = lax.axis_size(axes)
    got = lax.all_to_all(part.reshape(n, -1, part.shape[1]), axes, 0, 0, tiled=True)
    if n > 4:
        return jnp.sum(got.astype(f32), axis=0)
    total = got[0].astype(f32)
    for at in range(1, n):
        total = total + got[at].astype(f32)
    return total


def shards(tokens, cotangent, w_in, b_in, w_out):
    zh = lax.axis_index("zh")
    core = lax.axis_index("core")
    tok_dev, feat = tokens.shape
    quarter = w_in.shape[1]
    half_h = 2 * quarter
    quarter_d = w_out.shape[1]
    half_d = 2 * quarter_d

    kept = jnp.concatenate([tokens, part_of(cotangent, zh, half_d, 1)], 1)
    sent = jnp.concatenate([tokens, part_of(cotangent, 1 - zh, half_d, 1)], 1)
    got = swap(sent, "zh")
    w_out, w_in = after(got, w_out, w_in)
    out_pair = join(w_out, swap(w_out, "core"), "core", 1)
    in_pair = join(w_in, swap(w_in, "core"), "core", 1)
    in_pair, out_pair = after(got, in_pair, out_pair)
    rows = join(kept, got, "zh", 0)

    every_g = spread(rows[:, feat:], GRID)
    every_x = spread(after(every_g, rows[:, :feat]), GRID)

    back = against(every_g, out_pair).reshape(2, 2, -1, 2 * half_h)
    back_kept, back_sent = cut(back, "rl", 1)
    back_kept, back_sent = cut(back_kept + swap(back_sent, "rl").astype(f32), "rm", 0)
    every_x = after(back_sent, every_x)
    pre = dot(every_x, in_pair).astype(bf16)
    back = (back_kept + swap(back_sent, "rm").astype(f32))[0, 0]
    pre = deal(pre, ROW4).astype(bf16)

    back_kept, back_sent = cut(back, "zh", 1)
    back = (back_kept + after(pre, cross(back_sent)).astype(f32)).astype(bf16)
    pair_x = swap(every_x, "core")
    pair_g = swap(part_of(every_g, 1 - core, quarter_d, 1), "core")
    pre = after((pair_x, pair_g), pre)
    pre = pre.astype(f32) + swap(pre, "rh").astype(f32)
    back = back.astype(f32) + swap(back, "rh").astype(f32)

    act_f, slope = gelu_pair(pre + part_of(b_in, zh, half_h, 0))
    act = act_f.astype(bf16)
    act = join(act, cross(act), "zh", 1)[None, None]
    grad = spread((back * slope).astype(bf16), ROW4)
    part = against(grad, in_pair).astype(bf16)
    summed = deal(part, GRID)
    act = widen(after(part, act), "rm", 0)
    grad_sent = after(act, part_of(grad, 1 - core, quarter, 1))
    act = widen(act, "rl", 1).reshape(-1, act.shape[-1])
    out_rows = part_of(summed, 1 - zh, tok_dev, 0).astype(bf16)
    own_rows = part_of(summed, zh, tok_dev, 0)
    input_grad = (own_rows + swap(out_rows, "zh").astype(f32)).astype(bf16)

    own_grad = part_of(grad, core, quarter, 1)
    pair_grad = swap(grad_sent, "core")
    w_in_grad = (over_rows(every_x, own_grad) + over_rows(pair_x, pair_grad)).astype(bf16)
    b_in_grad = jnp.sum(own_grad.astype(f32), 0) + jnp.sum(pair_grad.astype(f32), 0)

    own_g = part_of(every_g, core, quarter_d, 1)
    pair_act = swap(act, "core")
    w_out_grad = (over_rows(act, own_g) + over_rows(pair_act, pair_g)).astype(bf16)
    return (input_grad, w_in_grad, b_in_grad, w_out_grad)


def solution(mesh):
    grid = Mesh(
        mesh.devices.reshape(2, 2, 2, 4, 4, 2, 2), ("rh", "rm", "rl", "x", "y", "zh", "core")
    )
    row, col, depth = ("rh", "rm", "rl"), ("x", "y"), ("zh", "core")
    return jax.shard_map(
        shards,
        mesh=grid,
        in_specs=(
            P(col + depth, row),
            P(col + depth, row),
            P(row, col + depth),
            P(col),
            P(col, row + depth),
        ),
        out_specs=(
            P(col + depth, row),
            P(row, col + depth),
            P(col + depth),
            P(col, row + depth),
        ),
        check_vma=False,
    )
```

```python
import jax
import jax.numpy as jnp
from jax import lax
from jax.sharding import Mesh, PartitionSpec as P

coef = 0.7978845608
bf16 = jnp.bfloat16
f32 = jnp.float32
SWAP = [(0, 1), (1, 0)]
CROSS = [(0, 3), (1, 2), (2, 1), (3, 0)]
GRID = ("x", "y")
ROW4 = ("rm", "rl")


def gelu_pair(pre):
    inner = coef * (pre + 0.044715 * pre * pre * pre)
    tanh_v = jnp.tanh(inner)
    act = 0.5 * pre * (1.0 + tanh_v)
    slope = 0.5 * (1.0 + tanh_v) + 0.5 * pre * (1.0 - tanh_v * tanh_v) * coef * (
        1.0 + 0.134145 * pre * pre
    )
    return (act, slope)


def dot(left, right):
    return jnp.dot(left, right, preferred_element_type=f32)


def against(left, right):
    return lax.dot_general(left, right, (((1,), (1,)), ((), ())), preferred_element_type=f32)


def over_rows(left, right):
    return lax.dot_general(left, right, (((0,), (0,)), ((), ())), preferred_element_type=f32)


def part_of(whole, at, size, dim):
    return lax.dynamic_slice_in_dim(whole, at * size, size, dim)


def swap(value, axis):
    return lax.ppermute(value, axis, SWAP)


def join(mine, other, axis, dim):
    first = lax.axis_index(axis) == 0
    return jnp.where(
        first,
        jnp.concatenate([mine, other], dim),
        jnp.concatenate([other, mine], dim),
    )


def after(first, *values):
    kept = lax.optimization_barrier((first, *values))[1:]
    return kept[0] if len(kept) == 1 else kept


def cut(part, axis, dim):
    size = part.shape[dim] // 2
    at = lax.axis_index(axis)
    return part_of(part, at, size, dim), part_of(part, 1 - at, size, dim).astype(bf16)


def cross(value):
    return lax.ppermute(value, ("rh", "zh"), CROSS)


def spread(rows, axes):
    n = lax.axis_size(axes)
    sent = jnp.broadcast_to(rows[None], (n,) + rows.shape)
    got = lax.all_to_all(sent, axes, 0, 0, tiled=True)
    return got.reshape(n * rows.shape[0], rows.shape[1])


def deal(part, axes):
    n = lax.axis_size(axes)
    got = lax.all_to_all(part.reshape(n, -1, part.shape[1]), axes, 0, 0, tiled=True)
    if n > 4:
        return jnp.sum(got.astype(f32), axis=0)
    total = got[0].astype(f32)
    for at in range(1, n):
        total = total + got[at].astype(f32)
    return total


def shards(tokens, cotangent, w_in, b_in, w_out):
    zh = lax.axis_index("zh")
    core = lax.axis_index("core")
    tok_dev, feat = tokens.shape
    quarter = w_in.shape[1]
    half_h = 2 * quarter
    quarter_d = w_out.shape[1]
    half_d = 2 * quarter_d

    kept = jnp.concatenate([tokens, part_of(cotangent, zh, half_d, 1)], 1)
    sent = jnp.concatenate([tokens, part_of(cotangent, 1 - zh, half_d, 1)], 1)
    got = swap(sent, "zh")
    rows = join(kept, got, "zh", 0)
    w_out = after(rows, w_out)
    out_pair = after(rows, join(w_out, swap(w_out, "core"), "core", 1))

    every_g = spread(rows[:, feat:], GRID)
    every_x = spread(after(every_g, rows[:, :feat]), GRID)
    w_in = after(every_g, w_in)
    in_pair = after(rows, join(w_in, swap(w_in, "core"), "core", 1))

    back = against(every_g, out_pair).reshape(2, 2, -1, 2 * half_h)
    back_kept, back_sent = cut(back, "rl", 1)
    back_kept, back_sent = cut(back_kept + swap(back_sent, "rl").astype(f32), "rm", 0)
    every_x = after(back_sent, every_x)
    pre = dot(every_x, in_pair).astype(bf16)
    back_got = swap(back_sent, "rm")
    pre = deal(after(back_got, pre), ROW4).astype(bf16)
    back_kept, back_sent = cut((back_kept + back_got.astype(f32))[0, 0], "zh", 1)
    back = (back_kept + cross(back_sent).astype(f32)).astype(bf16)
    pair_x = swap(every_x, "core")
    pair_g = swap(part_of(every_g, 1 - core, quarter_d, 1), "core")
    pre = after((pair_x, pair_g), pre)
    met = jnp.concatenate([pre, back], 1)
    met = met.astype(f32) + swap(met, "rh").astype(f32)
    pre, back = met[:, :half_h], met[:, half_h:]

    act_f, slope = gelu_pair(pre + part_of(b_in, zh, half_h, 0))
    act = act_f.astype(bf16)
    act = join(act, cross(act), "zh", 1)[None, None]
    grad = spread((back * slope).astype(bf16), ROW4)
    part = against(grad, in_pair).astype(bf16)
    summed = deal(part, GRID)
    act = join(act, after(part, swap(act, "rm")), "rm", 0)
    grad_sent = after(act, part_of(grad, 1 - core, quarter, 1))
    act = join(act, swap(act, "rl"), "rl", 1).reshape(-1, act.shape[-1])
    out_rows = part_of(summed, 1 - zh, tok_dev, 0).astype(bf16)
    own_rows = part_of(summed, zh, tok_dev, 0)

    own_grad = part_of(grad, core, quarter, 1)
    pair_grad = swap(grad_sent, "core")
    w_in_grad = (over_rows(every_x, own_grad) + over_rows(pair_x, pair_grad)).astype(bf16)
    b_in_grad = jnp.sum(own_grad.astype(f32), 0) + jnp.sum(pair_grad.astype(f32), 0)

    own_g = part_of(every_g, core, quarter_d, 1)
    pair_act = swap(act, "core")
    w_out_grad = (over_rows(act, own_g) + over_rows(pair_act, pair_g)).astype(bf16)
    got_rows = after(w_out_grad, swap(out_rows, "zh"))
    input_grad = (own_rows + got_rows.astype(f32)).astype(bf16)
    return (input_grad, w_in_grad, b_in_grad, w_out_grad)


def solution(mesh):
    grid = Mesh(
        mesh.devices.reshape(2, 2, 2, 4, 4, 2, 2), ("rh", "rm", "rl", "x", "y", "zh", "core")
    )
    row, col, depth = ("rh", "rm", "rl"), ("x", "y"), ("zh", "core")
    return jax.shard_map(
        shards,
        mesh=grid,
        in_specs=(
            P(col + depth, row),
            P(col + depth, row),
            P(row, col + depth),
            P(col),
            P(col, row + depth),
        ),
        out_specs=(
            P(col + depth, row),
            P(row, col + depth),
            P(col + depth),
            P(col, row + depth),
        ),
        check_vma=False,
    )
```

```python
import jax
import jax.numpy as jnp
from jax import lax
from jax.sharding import Mesh, PartitionSpec as P

coef = 0.7978845608
bf16 = jnp.bfloat16
f32 = jnp.float32
SWAP = [(0, 1), (1, 0)]
CROSS = [(0, 3), (1, 2), (2, 1), (3, 0)]
GRID = ("x", "y")
ROW4 = ("rm", "rl")


def gelu_pair(pre):
    inner = coef * (pre + 0.044715 * pre * pre * pre)
    tanh_v = jnp.tanh(inner)
    act = 0.5 * pre * (1.0 + tanh_v)
    slope = 0.5 * (1.0 + tanh_v) + 0.5 * pre * (1.0 - tanh_v * tanh_v) * coef * (
        1.0 + 0.134145 * pre * pre
    )
    return (act, slope)


def dot(left, right):
    return jnp.dot(left, right, preferred_element_type=f32)


def against(left, right):
    return lax.dot_general(left, right, (((1,), (1,)), ((), ())), preferred_element_type=f32)


def over_rows(left, right):
    return lax.dot_general(left, right, (((0,), (0,)), ((), ())), preferred_element_type=f32)


def part_of(whole, at, size, dim):
    return lax.dynamic_slice_in_dim(whole, at * size, size, dim)


def swap(value, axis):
    return lax.ppermute(value, axis, SWAP)


def join(mine, other, axis, dim):
    first = lax.axis_index(axis) == 0
    return jnp.where(
        first,
        jnp.concatenate([mine, other], dim),
        jnp.concatenate([other, mine], dim),
    )


def after(first, *values):
    kept = lax.optimization_barrier((first, *values))[1:]
    return kept[0] if len(kept) == 1 else kept


def cut(part, axis, dim):
    size = part.shape[dim] // 2
    at = lax.axis_index(axis)
    return part_of(part, at, size, dim), part_of(part, 1 - at, size, dim).astype(bf16)


def cross(value):
    return lax.ppermute(value, ("rh", "zh"), CROSS)


def spread(rows, axes):
    n = lax.axis_size(axes)
    sent = jnp.broadcast_to(rows[None], (n,) + rows.shape)
    got = lax.all_to_all(sent, axes, 0, 0, tiled=True)
    return got.reshape(n * rows.shape[0], rows.shape[1])


def deal(part, axes):
    n = lax.axis_size(axes)
    got = lax.all_to_all(part.reshape(n, -1, part.shape[1]), axes, 0, 0, tiled=True)
    total = got[0].astype(f32)
    for at in range(1, n):
        total = total + got[at].astype(f32)
    return total


def shards(tokens, cotangent, w_in, b_in, w_out):
    zh = lax.axis_index("zh")
    core = lax.axis_index("core")
    tok_dev, feat = tokens.shape
    quarter = w_in.shape[1]
    half_h = 2 * quarter
    quarter_d = w_out.shape[1]
    half_d = 2 * quarter_d

    kept = jnp.concatenate([tokens, part_of(cotangent, zh, half_d, 1)], 1)
    sent = jnp.concatenate([tokens, part_of(cotangent, 1 - zh, half_d, 1)], 1)
    got = swap(sent, "zh")
    rows = join(kept, got, "zh", 0)
    w_out = after(rows, w_out)
    out_pair = after(rows, join(w_out, swap(w_out, "core"), "core", 1))

    every_g = spread(rows[:, feat:], GRID)
    every_x = spread(after(every_g, rows[:, :feat]), GRID)

    back = against(every_g, out_pair).reshape(2, 2, -1, 2 * half_h)
    back_kept, back_sent = cut(back, "rl", 1)
    w_in = after(back_sent, w_in)
    in_pair = after(rows, join(w_in, swap(w_in, "core"), "core", 1))
    back_kept, back_sent = cut(back_kept + swap(back_sent, "rl").astype(f32), "rm", 0)
    every_x = after((back_sent, in_pair), every_x)
    pre = dot(every_x, in_pair).astype(bf16)
    back_got = swap(back_sent, "rm")
    pre = deal(after(back_got, pre), ROW4).astype(bf16)
    back_kept, back_sent = cut((back_kept + back_got.astype(f32))[0, 0], "zh", 1)
    back = (back_kept + cross(back_sent).astype(f32)).astype(bf16)
    pair_x = swap(every_x, "core")
    pair_g = swap(part_of(every_g, 1 - core, quarter_d, 1), "core")
    pre = after((pair_x, pair_g), pre)
    met = jnp.concatenate([pre, back], 1)
    met = met.astype(f32) + swap(met, "rh").astype(f32)
    pre, back = met[:, :half_h], met[:, half_h:]

    act_f, slope = gelu_pair(pre + part_of(b_in, zh, half_h, 0))
    act = act_f.astype(bf16)
    crossed = cross(act)
    grad = spread((back * slope).astype(bf16), ROW4)
    part = against(grad, in_pair).astype(bf16)
    dealt = lax.all_to_all(part.reshape(-1, 2 * tok_dev, feat), GRID, 0, 0, tiled=True)

    own_grad = part_of(grad, core, quarter, 1)
    act = join(act, after(part, crossed), "zh", 1)[None, None]
    act = join(act, swap(act, "rm"), "rm", 0)
    own_part = over_rows(every_x, own_grad)
    pair_grad = swap(after(act, part_of(grad, 1 - core, quarter, 1)), "core")
    act = join(act, swap(act, "rl"), "rl", 1).reshape(-1, act.shape[-1])
    w_in_grad = (own_part + over_rows(pair_x, pair_grad)).astype(bf16)
    b_in_grad = jnp.sum(own_grad.astype(f32), 0) + jnp.sum(pair_grad.astype(f32), 0)

    summed = jnp.sum(after((w_in_grad, b_in_grad), dealt).astype(f32), axis=0)
    out_rows = part_of(summed, 1 - zh, tok_dev, 0).astype(bf16)
    own_rows = part_of(summed, zh, tok_dev, 0)
    own_g = part_of(every_g, core, quarter_d, 1)
    pair_act = swap(after(out_rows, act), "core")
    w_out_grad = (over_rows(act, own_g) + over_rows(pair_act, pair_g)).astype(bf16)
    got_rows = after(w_out_grad, swap(out_rows, "zh"))
    input_grad = (own_rows + got_rows.astype(f32)).astype(bf16)
    return (input_grad, w_in_grad, b_in_grad, w_out_grad)


def solution(mesh):
    grid = Mesh(
        mesh.devices.reshape(2, 2, 2, 4, 4, 2, 2), ("rh", "rm", "rl", "x", "y", "zh", "core")
    )
    row, col, depth = ("rh", "rm", "rl"), ("x", "y"), ("zh", "core")
    return jax.shard_map(
        shards,
        mesh=grid,
        in_specs=(
            P(col + depth, row),
            P(col + depth, row),
            P(row, col + depth),
            P(col),
            P(col, row + depth),
        ),
        out_specs=(
            P(col + depth, row),
            P(row, col + depth),
            P(col + depth),
            P(col, row + depth),
        ),
        check_vma=False,
    )
```

```python
import jax
import jax.numpy as jnp
from jax import lax
from jax.sharding import Mesh, PartitionSpec as P

coef = 0.7978845608
bf16 = jnp.bfloat16
f32 = jnp.float32
SWAP = [(0, 1), (1, 0)]
CROSS = [(0, 3), (1, 2), (2, 1), (3, 0)]
GRID = ("x", "y")
ROW4 = ("rm", "rl")


def gelu_pair(pre):
    inner = coef * (pre + 0.044715 * pre * pre * pre)
    tanh_v = jnp.tanh(inner)
    act = 0.5 * pre * (1.0 + tanh_v)
    slope = 0.5 * (1.0 + tanh_v) + 0.5 * pre * (1.0 - tanh_v * tanh_v) * coef * (
        1.0 + 0.134145 * pre * pre
    )
    return (act, slope)


def dot(left, right):
    return jnp.dot(left, right, preferred_element_type=f32)


def against(left, right):
    return lax.dot_general(left, right, (((1,), (1,)), ((), ())), preferred_element_type=f32)


def over_rows(left, right):
    return lax.dot_general(left, right, (((0,), (0,)), ((), ())), preferred_element_type=f32)


def part_of(whole, at, size, dim):
    return lax.dynamic_slice_in_dim(whole, at * size, size, dim)


def swap(value, axis):
    return lax.ppermute(value, axis, SWAP)


def join(mine, other, axis, dim):
    first = lax.axis_index(axis) == 0
    return jnp.where(
        first,
        jnp.concatenate([mine, other], dim),
        jnp.concatenate([other, mine], dim),
    )


def after(first, *values):
    kept = lax.optimization_barrier((first, *values))[1:]
    return kept[0] if len(kept) == 1 else kept


def cut(part, axis, dim):
    size = part.shape[dim] // 2
    at = lax.axis_index(axis)
    return part_of(part, at, size, dim), part_of(part, 1 - at, size, dim).astype(bf16)


def cross(value):
    return lax.ppermute(value, ("rh", "zh"), CROSS)


def spread(rows, axes):
    n = lax.axis_size(axes)
    sent = jnp.broadcast_to(rows[None], (n,) + rows.shape)
    got = lax.all_to_all(sent, axes, 0, 0, tiled=True)
    return got.reshape(n * rows.shape[0], rows.shape[1])


def deal(part, axes):
    n = lax.axis_size(axes)
    got = lax.all_to_all(part.reshape(n, -1, part.shape[1]), axes, 0, 0, tiled=True)
    total = got[0].astype(f32)
    for at in range(1, n):
        total = total + got[at].astype(f32)
    return total


def shards(tokens, cotangent, w_in, b_in, w_out):
    zh = lax.axis_index("zh")
    core = lax.axis_index("core")
    tok_dev, feat = tokens.shape
    quarter = w_in.shape[1]
    half_h = 2 * quarter
    quarter_d = w_out.shape[1]
    half_d = 2 * quarter_d

    kept = jnp.concatenate([tokens, part_of(cotangent, zh, half_d, 1)], 1)
    sent = jnp.concatenate([tokens, part_of(cotangent, 1 - zh, half_d, 1)], 1)
    got = swap(sent, "zh")
    rows = join(kept, got, "zh", 0)
    w_out = after(rows, w_out)
    out_pair = after(rows, join(w_out, swap(w_out, "core"), "core", 1))
    w_in = after(out_pair, w_in)
    in_pair = after(rows, join(w_in, swap(w_in, "core"), "core", 1))

    every_g = spread(rows[:, feat:], GRID)
    every_x = spread(after(every_g, rows[:, :feat]), GRID)

    back = against(every_g, out_pair).reshape(2, 2, -1, 2 * half_h)
    back_kept, back_sent = cut(back, "rl", 1)
    back_kept, back_sent = cut(back_kept + swap(back_sent, "rl").astype(f32), "rm", 0)
    every_x = after((back_sent, in_pair), every_x)
    pre = dot(every_x, in_pair).astype(bf16)
    back_got = swap(back_sent, "rm")
    pre = deal(after(back_got, pre), ROW4).astype(bf16)
    back_kept, back_sent = cut((back_kept + back_got.astype(f32))[0, 0], "zh", 1)
    pre_got = swap(pre, "rh")
    back = (back_kept + after(pre_got, cross(back_sent)).astype(f32)).astype(bf16)
    pre = pre.astype(f32) + pre_got.astype(f32)
    act_f, slope = gelu_pair(pre + part_of(b_in, zh, half_h, 0))
    act, slope = lax.optimization_barrier((act_f.astype(bf16), slope))
    crossed = cross(act)
    pair_x = swap(after(back, every_x), "core")
    pair_g = part_of(every_g, 1 - core, quarter_d, 1)
    pair_g = swap(after(back, pair_g), "core")
    back_got = after((act, pair_x, pair_g), swap(back, "rh"))
    back = back.astype(f32) + back_got.astype(f32)

    grad = spread((back * slope).astype(bf16), ROW4)
    part = against(grad, in_pair).astype(bf16)
    dealt = lax.all_to_all(part.reshape(-1, 2 * tok_dev, feat), GRID, 0, 0, tiled=True)

    own_grad = part_of(grad, core, quarter, 1)
    act = join(act, after(part, crossed), "zh", 1)[None, None]
    act = join(act, swap(act, "rm"), "rm", 0)
    own_part = over_rows(every_x, own_grad)
    pair_grad = swap(after(act, part_of(grad, 1 - core, quarter, 1)), "core")
    act = join(act, swap(act, "rl"), "rl", 1).reshape(-1, act.shape[-1])
    w_in_grad = (own_part + over_rows(pair_x, pair_grad)).astype(bf16)
    b_in_grad = jnp.sum(own_grad.astype(f32), 0) + jnp.sum(pair_grad.astype(f32), 0)

    summed = jnp.sum(after((w_in_grad, b_in_grad), dealt).astype(f32), axis=0)
    out_rows = part_of(summed, 1 - zh, tok_dev, 0).astype(bf16)
    own_rows = part_of(summed, zh, tok_dev, 0)
    own_g = part_of(every_g, core, quarter_d, 1)
    pair_act = swap(after(out_rows, act), "core")
    w_out_grad = (over_rows(act, own_g) + over_rows(pair_act, pair_g)).astype(bf16)
    got_rows = after(w_out_grad, swap(out_rows, "zh"))
    input_grad = (own_rows + got_rows.astype(f32)).astype(bf16)
    return (input_grad, w_in_grad, b_in_grad, w_out_grad)


def solution(mesh):
    grid = Mesh(
        mesh.devices.reshape(2, 2, 2, 4, 4, 2, 2), ("rh", "rm", "rl", "x", "y", "zh", "core")
    )
    row, col, depth = ("rh", "rm", "rl"), ("x", "y"), ("zh", "core")
    return jax.shard_map(
        shards,
        mesh=grid,
        in_specs=(
            P(col + depth, row),
            P(col + depth, row),
            P(row, col + depth),
            P(col),
            P(col, row + depth),
        ),
        out_specs=(
            P(col + depth, row),
            P(row, col + depth),
            P(col + depth),
            P(col, row + depth),
        ),
        check_vma=False,
    )
```

```python
import jax
import jax.numpy as jnp
from jax import lax
from jax.sharding import Mesh, PartitionSpec as P

coef = 0.7978845608
bf16 = jnp.bfloat16
f32 = jnp.float32
SWAP = [(0, 1), (1, 0)]
CROSS = [(0, 3), (1, 2), (2, 1), (3, 0)]
GRID = ("x", "y")
ROW4 = ("rm", "rl")


def gelu_pair(pre):
    inner = coef * (pre + 0.044715 * pre * pre * pre)
    tanh_v = jnp.tanh(inner)
    act = 0.5 * pre * (1.0 + tanh_v)
    slope = 0.5 * (1.0 + tanh_v) + 0.5 * pre * (1.0 - tanh_v * tanh_v) * coef * (
        1.0 + 0.134145 * pre * pre
    )
    return (act, slope)


def dot(left, right):
    return jnp.dot(left, right, preferred_element_type=f32)


def against(left, right):
    return lax.dot_general(left, right, (((1,), (1,)), ((), ())), preferred_element_type=f32)


def over_rows(left, right):
    return lax.dot_general(left, right, (((0,), (0,)), ((), ())), preferred_element_type=f32)


def part_of(whole, at, size, dim):
    return lax.dynamic_slice_in_dim(whole, at * size, size, dim)


def swap(value, axis):
    return lax.ppermute(value, axis, SWAP)


def joined(at, mine, other, dim):
    return jnp.where(
        at == 0,
        jnp.concatenate([mine, other], dim),
        jnp.concatenate([other, mine], dim),
    )


def join(mine, other, axis, dim):
    return joined(lax.axis_index(axis), mine, other, dim)


def after(first, *values):
    kept = lax.optimization_barrier((first, *values))[1:]
    return kept[0] if len(kept) == 1 else kept


def cut(part, axis, dim):
    size = part.shape[dim] // 2
    at = lax.axis_index(axis)
    return part_of(part, at, size, dim), part_of(part, 1 - at, size, dim).astype(bf16)


def cross(value):
    return lax.ppermute(value, ("rh", "zh"), CROSS)


def spread(rows, axes):
    n = lax.axis_size(axes)
    sent = jnp.broadcast_to(rows[None], (n,) + rows.shape)
    got = lax.all_to_all(sent, axes, 0, 0, tiled=True)
    return got.reshape(n * rows.shape[0], rows.shape[1])


def deal(part, axes):
    n = lax.axis_size(axes)
    got = lax.all_to_all(part.reshape(n, -1, part.shape[1]), axes, 0, 0, tiled=True)
    total = got[0].astype(f32)
    for at in range(1, n):
        total = total + got[at].astype(f32)
    return total


def shards(tokens, cotangent, w_in, b_in, w_out):
    zh = lax.axis_index("zh")
    core = lax.axis_index("core")
    tok_dev, feat = tokens.shape
    quarter = w_in.shape[1]
    half_h = 2 * quarter
    quarter_d = w_out.shape[1]
    half_d = 2 * quarter_d

    kept = jnp.concatenate([tokens, part_of(cotangent, zh, half_d, 1)], 1)
    sent = jnp.concatenate([tokens, part_of(cotangent, 1 - zh, half_d, 1)], 1)
    got = swap(sent, "zh")
    rows = join(kept, got, "zh", 0)
    w_out = after(rows, w_out)
    out_pair = after(rows, join(w_out, swap(w_out, "core"), "core", 1))
    w_in = after(out_pair, w_in)
    in_pair = after(rows, join(w_in, swap(w_in, "core"), "core", 1))

    every_g = spread(rows[:, feat:], GRID)
    every_x = spread(after(every_g, rows[:, :feat]), GRID)

    back = against(every_g, out_pair).reshape(2, 2, -1, 2 * half_h)
    back_kept, back_sent = cut(back, "rl", 1)
    back_kept, back_sent = cut(back_kept + swap(back_sent, "rl").astype(f32), "rm", 0)
    every_x = after((back_sent, in_pair), every_x)
    pre = dot(every_x, in_pair).astype(bf16)
    back_got = swap(back_sent, "rm")
    pre = deal(after(back_got, pre), ROW4)
    back = (back_kept + back_got.astype(f32))[0, 0]
    side = (lax.axis_index("rh") + zh) % 2
    n_rows = back.shape[0] // 2
    back_sent = part_of(back, 1 - side, n_rows, 0).astype(bf16)
    back_half = part_of(back, side, n_rows, 0) + swap(back_sent, "rh").astype(f32)
    back_kept, back_sent = cut(back_half, "zh", 1)
    pre_got = swap(part_of(pre, 1 - side, n_rows, 0).astype(bf16), "rh")
    pre = part_of(pre, side, n_rows, 0) + pre_got.astype(f32)
    back = back_kept + after(pre_got, cross(back_sent)).astype(f32)

    act_f, slope = gelu_pair(pre + part_of(b_in, zh, half_h, 0))
    act, slope = lax.optimization_barrier((act_f.astype(bf16), slope))
    crossed = cross(act)
    grad = (back * slope).astype(bf16)
    grad = joined(side, grad, swap(grad, "rh"), 0)
    act = join(act, after(grad, crossed), "zh", 1)
    act_got = swap(act, "rh")
    pair_x = swap(after(grad, every_x), "core")
    pair_g = part_of(every_g, 1 - core, quarter_d, 1)
    pair_g = swap(after(grad, pair_g), "core")
    grad = after((pair_x, pair_g), spread(grad, ROW4))
    part = against(grad, in_pair).astype(bf16)
    dealt = lax.all_to_all(part.reshape(-1, 2 * tok_dev, feat), GRID, 0, 0, tiled=True)

    own_grad = part_of(grad, core, quarter, 1)
    act = joined(side, act, after(part, act_got), 0)[None, None]
    act = join(act, swap(act, "rm"), "rm", 0)
    own_part = over_rows(every_x, after(act, own_grad))
    pair_grad = swap(after(act, part_of(grad, 1 - core, quarter, 1)), "core")
    act = join(act, swap(act, "rl"), "rl", 1).reshape(-1, act.shape[-1])
    w_in_grad = (own_part + over_rows(pair_x, pair_grad)).astype(bf16)
    b_in_grad = jnp.sum(own_grad.astype(f32), 0) + jnp.sum(pair_grad.astype(f32), 0)

    summed = jnp.sum(after((w_in_grad, b_in_grad), dealt).astype(f32), axis=0)
    out_rows = part_of(summed, 1 - zh, tok_dev, 0).astype(bf16)
    own_rows = part_of(summed, zh, tok_dev, 0)
    own_g = part_of(every_g, core, quarter_d, 1)
    pair_act = swap(after(out_rows, act), "core")
    w_out_grad = (over_rows(act, own_g) + over_rows(pair_act, pair_g)).astype(bf16)
    got_rows = after(w_out_grad, swap(out_rows, "zh"))
    input_grad = (own_rows + got_rows.astype(f32)).astype(bf16)
    return (input_grad, w_in_grad, b_in_grad, w_out_grad)


def solution(mesh):
    grid = Mesh(
        mesh.devices.reshape(2, 2, 2, 4, 4, 2, 2), ("rh", "rm", "rl", "x", "y", "zh", "core")
    )
    row, col, depth = ("rh", "rm", "rl"), ("x", "y"), ("zh", "core")
    return jax.shard_map(
        shards,
        mesh=grid,
        in_specs=(
            P(col + depth, row),
            P(col + depth, row),
            P(row, col + depth),
            P(col),
            P(col, row + depth),
        ),
        out_specs=(
            P(col + depth, row),
            P(row, col + depth),
            P(col + depth),
            P(col, row + depth),
        ),
        check_vma=False,
    )
```

```python
import jax
import jax.numpy as jnp
from jax import lax
from jax.sharding import Mesh, PartitionSpec as P

coef = 0.7978845608
bf16 = jnp.bfloat16
f32 = jnp.float32
SWAP = [(0, 1), (1, 0)]
CROSS = [(0, 3), (1, 2), (2, 1), (3, 0)]
GRID = ("x", "y")
ROW4 = ("rm", "rl")


def gelu_pair(pre):
    inner = coef * (pre + 0.044715 * pre * pre * pre)
    tanh_v = jnp.tanh(inner)
    act = 0.5 * pre * (1.0 + tanh_v)
    slope = 0.5 * (1.0 + tanh_v) + 0.5 * pre * (1.0 - tanh_v * tanh_v) * coef * (
        1.0 + 0.134145 * pre * pre
    )
    return (act, slope)


def dot(left, right):
    return jnp.dot(left, right, preferred_element_type=f32)


def against(left, right):
    return lax.dot_general(left, right, (((1,), (1,)), ((), ())), preferred_element_type=f32)


def over_rows(left, right):
    return lax.dot_general(left, right, (((0,), (0,)), ((), ())), preferred_element_type=f32)


def part_of(whole, at, size, dim):
    return lax.dynamic_slice_in_dim(whole, at * size, size, dim)


def swap(value, axis):
    return lax.ppermute(value, axis, SWAP)


def join(mine, other, axis, dim):
    first = lax.axis_index(axis) == 0
    return jnp.where(
        first,
        jnp.concatenate([mine, other], dim),
        jnp.concatenate([other, mine], dim),
    )


def after(first, *values):
    kept = lax.optimization_barrier((first, *values))[1:]
    return kept[0] if len(kept) == 1 else kept


def cut(part, axis, dim):
    size = part.shape[dim] // 2
    at = lax.axis_index(axis)
    return part_of(part, at, size, dim), part_of(part, 1 - at, size, dim).astype(bf16)


def cross(value):
    return lax.ppermute(value, ("rh", "zh"), CROSS)


def spread(rows, axes):
    n = lax.axis_size(axes)
    sent = jnp.broadcast_to(rows[None], (n,) + rows.shape)
    got = lax.all_to_all(sent, axes, 0, 0, tiled=True)
    return got.reshape(n * rows.shape[0], rows.shape[1])


def deal(part, axes):
    n = lax.axis_size(axes)
    got = lax.all_to_all(part.reshape(n, -1, part.shape[1]), axes, 0, 0, tiled=True)
    total = got[0].astype(f32)
    for at in range(1, n):
        total = total + got[at].astype(f32)
    return total


def shards(tokens, cotangent, w_in, b_in, w_out):
    zh = lax.axis_index("zh")
    core = lax.axis_index("core")
    tok_dev, feat = tokens.shape
    quarter = w_in.shape[1]
    half_h = 2 * quarter
    quarter_d = w_out.shape[1]
    half_d = 2 * quarter_d

    kept = jnp.concatenate([tokens, part_of(cotangent, zh, half_d, 1)], 1)
    sent = jnp.concatenate([tokens, part_of(cotangent, 1 - zh, half_d, 1)], 1)
    got = swap(sent, "zh")
    rows = join(kept, got, "zh", 0)
    w_out = after(rows, w_out)
    out_pair = after(rows, join(w_out, swap(w_out, "core"), "core", 1))

    every_g = spread(rows[:, feat:], GRID)
    every_x = spread(after(every_g, rows[:, :feat]), GRID)

    back = against(every_g, out_pair).reshape(2, 2, -1, 2 * half_h)
    back_kept, back_sent = cut(back, "rl", 1)
    w_in = after(back_sent, w_in)
    in_pair = after(rows, join(w_in, swap(w_in, "core"), "core", 1))
    back_kept, back_sent = cut(back_kept + swap(back_sent, "rl").astype(f32), "rm", 0)
    every_x = after((back_sent, in_pair), every_x)
    pre = dot(every_x, in_pair).astype(bf16)
    back_got = swap(back_sent, "rm")
    pre = deal(after(back_got, pre), ROW4).astype(bf16)
    back_kept, back_sent = cut((back_kept + back_got.astype(f32))[0, 0], "zh", 1)
    back = (back_kept + cross(back_sent).astype(f32)).astype(bf16)
    pair_x = swap(every_x, "core")
    pair_g = swap(part_of(every_g, 1 - core, quarter_d, 1), "core")
    pre = after((pair_x, pair_g), pre)
    met = jnp.concatenate([pre, back], 1)
    met = met.astype(f32) + swap(met, "rh").astype(f32)
    pre, back = met[:, :half_h], met[:, half_h:]

    act_f, slope = gelu_pair(pre + part_of(b_in, zh, half_h, 0))
    act = act_f.astype(bf16)
    crossed = cross(act)
    grad = spread((back * slope).astype(bf16), ROW4)
    part = against(grad, in_pair).astype(bf16)
    dealt = lax.all_to_all(part.reshape(-1, 2 * tok_dev, feat), GRID, 0, 0, tiled=True)

    own_grad = part_of(grad, core, quarter, 1)
    act = join(act, crossed, "zh", 1)[None, None]
    act = join(act, after(part, swap(act, "rm")), "rm", 0)
    own_part = over_rows(every_x, own_grad)
    pair_grad = swap(after(own_part, part_of(grad, 1 - core, quarter, 1)), "core")
    act = join(act, after(dealt, swap(after(own_part, act), "rl")), "rl", 1).reshape(-1, act.shape[-1])
    w_in_grad = (own_part + over_rows(pair_x, pair_grad)).astype(bf16)
    b_in_grad = jnp.sum(own_grad.astype(f32), 0) + jnp.sum(pair_grad.astype(f32), 0)

    summed = jnp.sum(after((w_in_grad, b_in_grad), dealt).astype(f32), axis=0)
    out_rows = part_of(summed, 1 - zh, tok_dev, 0).astype(bf16)
    own_rows = part_of(summed, zh, tok_dev, 0)
    own_g = part_of(every_g, core, quarter_d, 1)
    pair_act = swap(after(out_rows, act), "core")
    w_out_grad = (over_rows(act, own_g) + over_rows(pair_act, pair_g)).astype(bf16)
    got_rows = after(w_out_grad, swap(out_rows, "zh"))
    input_grad = (own_rows + got_rows.astype(f32)).astype(bf16)
    return (input_grad, w_in_grad, b_in_grad, w_out_grad)


def solution(mesh):
    grid = Mesh(
        mesh.devices.reshape(2, 2, 2, 4, 4, 2, 2), ("rh", "rm", "rl", "x", "y", "zh", "core")
    )
    row, col, depth = ("rh", "rm", "rl"), ("x", "y"), ("zh", "core")
    return jax.shard_map(
        shards,
        mesh=grid,
        in_specs=(
            P(col + depth, row),
            P(col + depth, row),
            P(row, col + depth),
            P(col),
            P(col, row + depth),
        ),
        out_specs=(
            P(col + depth, row),
            P(row, col + depth),
            P(col + depth),
            P(col, row + depth),
        ),
        check_vma=False,
    )
```

```python
import jax
import jax.numpy as jnp
from jax import lax
from jax.sharding import Mesh, PartitionSpec as P

coef = 0.7978845608
bf16 = jnp.bfloat16
f32 = jnp.float32
SWAP = [(0, 1), (1, 0)]
CROSS = [(0, 3), (1, 2), (2, 1), (3, 0)]
GRID = ("x", "y")
ROW4 = ("rm", "rl")


def gelu_pair(pre):
    inner = coef * (pre + 0.044715 * pre * pre * pre)
    tanh_v = jnp.tanh(inner)
    act = 0.5 * pre * (1.0 + tanh_v)
    slope = 0.5 * (1.0 + tanh_v) + 0.5 * pre * (1.0 - tanh_v * tanh_v) * coef * (
        1.0 + 0.134145 * pre * pre
    )
    return (act, slope)


def dot(left, right):
    return jnp.dot(left, right, preferred_element_type=f32)


def against(left, right):
    return lax.dot_general(left, right, (((1,), (1,)), ((), ())), preferred_element_type=f32)


def over_rows(left, right):
    return lax.dot_general(left, right, (((0,), (0,)), ((), ())), preferred_element_type=f32)


def part_of(whole, at, size, dim):
    return lax.dynamic_slice_in_dim(whole, at * size, size, dim)


def swap(value, axis):
    return lax.ppermute(value, axis, SWAP)


def join(mine, other, axis, dim):
    first = lax.axis_index(axis) == 0
    return jnp.where(
        first,
        jnp.concatenate([mine, other], dim),
        jnp.concatenate([other, mine], dim),
    )


def after(first, *values):
    kept = lax.optimization_barrier((first, *values))[1:]
    return kept[0] if len(kept) == 1 else kept


def cut(part, axis, dim):
    size = part.shape[dim] // 2
    at = lax.axis_index(axis)
    return part_of(part, at, size, dim), part_of(part, 1 - at, size, dim).astype(bf16)


def cross(value):
    return lax.ppermute(value, ("rh", "zh"), CROSS)


def spread(rows, axes):
    n = lax.axis_size(axes)
    sent = jnp.broadcast_to(rows[None], (n,) + rows.shape)
    got = lax.all_to_all(sent, axes, 0, 0, tiled=True)
    return got.reshape(n * rows.shape[0], rows.shape[1])


def deal(part, axes):
    n = lax.axis_size(axes)
    got = lax.all_to_all(part.reshape(n, -1, part.shape[1]), axes, 0, 0, tiled=True)
    total = got[0].astype(f32)
    for at in range(1, n):
        total = total + got[at].astype(f32)
    return total


def shards(tokens, cotangent, w_in, b_in, w_out):
    zh = lax.axis_index("zh")
    core = lax.axis_index("core")
    tok_dev, feat = tokens.shape
    quarter = w_in.shape[1]
    half_h = 2 * quarter
    quarter_d = w_out.shape[1]
    half_d = 2 * quarter_d

    kept = jnp.concatenate([tokens, part_of(cotangent, zh, half_d, 1)], 1)
    sent = jnp.concatenate([tokens, part_of(cotangent, 1 - zh, half_d, 1)], 1)
    got = swap(sent, "zh")
    rows = join(kept, got, "zh", 0)
    w_out = after(rows, w_out)
    out_pair = after(rows, join(w_out, swap(w_out, "core"), "core", 1))

    every_g = spread(rows[:, feat:], GRID)
    every_x = spread(after(every_g, rows[:, :feat]), GRID)

    back = against(every_g, out_pair).reshape(2, 2, -1, 2 * half_h)
    back_kept, back_sent = cut(back, "rl", 1)
    w_in = after(back_sent, w_in)
    in_pair = after(rows, join(w_in, swap(w_in, "core"), "core", 1))
    back_kept, back_sent = cut(back_kept + swap(back_sent, "rl").astype(f32), "rm", 0)
    every_x = after((back_sent, in_pair), every_x)
    pre = dot(every_x, in_pair).astype(bf16)
    back_got = swap(back_sent, "rm")
    pre = deal(after(back_got, pre), ROW4).astype(bf16)
    back_kept, back_sent = cut((back_kept + back_got.astype(f32))[0, 0], "zh", 1)
    back = (back_kept + cross(back_sent).astype(f32)).astype(bf16)
    pair_x = swap(every_x, "core")
    pair_g = swap(part_of(every_g, 1 - core, quarter_d, 1), "core")
    pre = after((pair_x, pair_g), pre)
    met = jnp.concatenate([pre, back], 1)
    met = met.astype(f32) + swap(met, "rh").astype(f32)
    pre, back = met[:, :half_h], met[:, half_h:]

    act_f, slope = gelu_pair(pre + part_of(b_in, zh, half_h, 0))
    act = act_f.astype(bf16)
    crossed = cross(act)
    grad = spread((back * slope).astype(bf16), ROW4)
    part = against(grad, in_pair).astype(bf16)
    dealt = lax.all_to_all(part.reshape(-1, 2 * tok_dev, feat), GRID, 0, 0, tiled=True)

    own_grad = part_of(grad, core, quarter, 1)
    act = join(act, after(part, crossed), "zh", 1)[None, None]
    act = join(act, swap(act, "rm"), "rm", 0)
    own_part = over_rows(every_x, own_grad)
    pair_grad = swap(after(act, part_of(grad, 1 - core, quarter, 1)), "core")
    rest = swap(act, "rl")
    pair_act = swap(act, "core")
    w_in_grad = (own_part + over_rows(pair_x, pair_grad)).astype(bf16)
    b_in_grad = jnp.sum(own_grad.astype(f32), 0) + jnp.sum(pair_grad.astype(f32), 0)

    summed = jnp.sum(after((w_in_grad, b_in_grad), dealt).astype(f32), axis=0)
    out_rows = part_of(summed, 1 - zh, tok_dev, 0).astype(bf16)
    own_rows = part_of(summed, zh, tok_dev, 0)
    got_rows = swap(out_rows, "zh")
    input_grad = (own_rows + got_rows.astype(f32)).astype(bf16)

    rl = lax.axis_index("rl")

    def rows_of(value, at):
        value = value.reshape(2, 2, -1, value.shape[-1])
        return part_of(value, at, 1, 1).reshape(-1, value.shape[-1])

    def flat(value):
        return value.reshape(-1, value.shape[-1])

    own_g = part_of(every_g, core, quarter_d, 1)
    w_out_sum = over_rows(flat(act), rows_of(own_g, rl)) + over_rows(flat(pair_act), rows_of(pair_g, rl))
    rest = flat(after(got_rows, rest))
    pair_rest = swap(rest, "core")
    w_out_sum = w_out_sum + over_rows(rest, rows_of(own_g, 1 - rl))
    w_out_grad = (w_out_sum + over_rows(pair_rest, rows_of(pair_g, 1 - rl))).astype(bf16)
    return (input_grad, w_in_grad, b_in_grad, w_out_grad)


def solution(mesh):
    grid = Mesh(
        mesh.devices.reshape(2, 2, 2, 4, 4, 2, 2), ("rh", "rm", "rl", "x", "y", "zh", "core")
    )
    row, col, depth = ("rh", "rm", "rl"), ("x", "y"), ("zh", "core")
    return jax.shard_map(
        shards,
        mesh=grid,
        in_specs=(
            P(col + depth, row),
            P(col + depth, row),
            P(row, col + depth),
            P(col),
            P(col, row + depth),
        ),
        out_specs=(
            P(col + depth, row),
            P(row, col + depth),
            P(col + depth),
            P(col, row + depth),
        ),
        check_vma=False,
    )
```

```python
import jax
import jax.numpy as jnp
from jax import lax
from jax.sharding import Mesh, PartitionSpec as P

coef = 0.7978845608
bf16 = jnp.bfloat16
f32 = jnp.float32
SWAP = [(0, 1), (1, 0)]
CROSS = [(0, 3), (1, 2), (2, 1), (3, 0)]
GRID = ("x", "y")
ROW4 = ("rm", "rl")


def gelu_pair(pre):
    inner = coef * (pre + 0.044715 * pre * pre * pre)
    tanh_v = jnp.tanh(inner)
    act = 0.5 * pre * (1.0 + tanh_v)
    slope = 0.5 * (1.0 + tanh_v) + 0.5 * pre * (1.0 - tanh_v * tanh_v) * coef * (
        1.0 + 0.134145 * pre * pre
    )
    return (act, slope)


def dot(left, right):
    return jnp.dot(left, right, preferred_element_type=f32)


def against(left, right):
    return lax.dot_general(left, right, (((1,), (1,)), ((), ())), preferred_element_type=f32)


def over_rows(left, right):
    return lax.dot_general(left, right, (((0,), (0,)), ((), ())), preferred_element_type=f32)


def part_of(whole, at, size, dim):
    return lax.dynamic_slice_in_dim(whole, at * size, size, dim)


def swap(value, axis):
    return lax.ppermute(value, axis, SWAP)


def join(mine, other, axis, dim):
    first = lax.axis_index(axis) == 0
    return jnp.where(
        first,
        jnp.concatenate([mine, other], dim),
        jnp.concatenate([other, mine], dim),
    )


def after(first, *values):
    kept = lax.optimization_barrier((first, *values))[1:]
    return kept[0] if len(kept) == 1 else kept


def cut(part, axis, dim):
    size = part.shape[dim] // 2
    at = lax.axis_index(axis)
    return part_of(part, at, size, dim), part_of(part, 1 - at, size, dim).astype(bf16)


def cross(value):
    return lax.ppermute(value, ("rh", "zh"), CROSS)


def spread(rows, axes):
    n = lax.axis_size(axes)
    sent = jnp.broadcast_to(rows[None], (n,) + rows.shape)
    got = lax.all_to_all(sent, axes, 0, 0, tiled=True)
    return got.reshape(n * rows.shape[0], rows.shape[1])


def deal(part, axes):
    n = lax.axis_size(axes)
    got = lax.all_to_all(part.reshape(n, -1, part.shape[1]), axes, 0, 0, tiled=True)
    total = got[0].astype(f32)
    for at in range(1, n):
        total = total + got[at].astype(f32)
    return total


def shards(tokens, cotangent, w_in, b_in, w_out):
    zh = lax.axis_index("zh")
    core = lax.axis_index("core")
    tok_dev, feat = tokens.shape
    quarter = w_in.shape[1]
    half_h = 2 * quarter
    quarter_d = w_out.shape[1]
    half_d = 2 * quarter_d

    kept = jnp.concatenate([tokens, part_of(cotangent, zh, half_d, 1)], 1)
    sent = jnp.concatenate([tokens, part_of(cotangent, 1 - zh, half_d, 1)], 1)
    got = swap(sent, "zh")
    rows = join(kept, got, "zh", 0)
    w_out = after(rows, w_out)
    out_pair = after(rows, join(w_out, swap(w_out, "core"), "core", 1))

    every_g = spread(rows[:, feat:], GRID)
    every_x = spread(after(every_g, rows[:, :feat]), GRID)

    back = against(every_g, out_pair).reshape(2, 2, -1, 2 * half_h)
    back_kept, back_sent = cut(back, "rl", 1)
    w_in = after(back_sent, w_in)
    in_pair = after(rows, join(w_in, swap(w_in, "core"), "core", 1))
    back_kept, back_sent = cut(back_kept + swap(back_sent, "rl").astype(f32), "rm", 0)
    every_x = after((back_sent, in_pair), every_x)
    pre = dot(every_x, in_pair).astype(bf16)
    back_got = swap(back_sent, "rm")
    pre = deal(after(back_got, pre), ROW4).astype(bf16)
    back_kept, back_sent = cut((back_kept + back_got.astype(f32))[0, 0], "zh", 1)
    back = (back_kept + cross(back_sent).astype(f32)).astype(bf16)
    met = jnp.concatenate([pre, back], 1)
    met = met.astype(f32) + swap(met, "rh").astype(f32)
    pre, back = met[:, :half_h], met[:, half_h:]

    act_f, slope = gelu_pair(pre + part_of(b_in, zh, half_h, 0))
    act = act_f.astype(bf16)
    crossed = cross(act)
    pair_x = swap(after(act, every_x), "core")
    pair_g = swap(after(act, part_of(every_g, 1 - core, quarter_d, 1)), "core")
    grad = spread((back * slope).astype(bf16), ROW4)
    grad = after((pair_x, pair_g), grad)
    part = against(grad, in_pair).astype(bf16)
    dealt = lax.all_to_all(part.reshape(-1, 2 * tok_dev, feat), GRID, 0, 0, tiled=True)

    own_grad = part_of(grad, core, quarter, 1)
    act = join(act, after(part, crossed), "zh", 1)[None, None]
    act = join(act, swap(act, "rm"), "rm", 0)
    own_part = over_rows(every_x, after(act, own_grad))
    pair_grad = swap(after(act, part_of(grad, 1 - core, quarter, 1)), "core")
    act = join(act, swap(after(own_part, act), "rl"), "rl", 1).reshape(-1, act.shape[-1])
    w_in_grad = (own_part + over_rows(pair_x, pair_grad)).astype(bf16)
    b_in_grad = jnp.sum(own_grad.astype(f32), 0) + jnp.sum(pair_grad.astype(f32), 0)

    summed = jnp.sum(after((w_in_grad, b_in_grad), dealt).astype(f32), axis=0)
    out_rows = part_of(summed, 1 - zh, tok_dev, 0).astype(bf16)
    own_rows = part_of(summed, zh, tok_dev, 0)
    own_g = part_of(every_g, core, quarter_d, 1)
    pair_act = swap(after(out_rows, act), "core")
    w_out_grad = (over_rows(act, own_g) + over_rows(pair_act, pair_g)).astype(bf16)
    got_rows = after(w_out_grad, swap(out_rows, "zh"))
    input_grad = (own_rows + got_rows.astype(f32)).astype(bf16)
    return (input_grad, w_in_grad, b_in_grad, w_out_grad)


def solution(mesh):
    grid = Mesh(
        mesh.devices.reshape(2, 2, 2, 4, 4, 2, 2), ("rh", "rm", "rl", "x", "y", "zh", "core")
    )
    row, col, depth = ("rh", "rm", "rl"), ("x", "y"), ("zh", "core")
    return jax.shard_map(
        shards,
        mesh=grid,
        in_specs=(
            P(col + depth, row),
            P(col + depth, row),
            P(row, col + depth),
            P(col),
            P(col, row + depth),
        ),
        out_specs=(
            P(col + depth, row),
            P(row, col + depth),
            P(col + depth),
            P(col, row + depth),
        ),
        check_vma=False,
    )
```

```python
import jax
import jax.numpy as jnp
from jax import lax
from jax.sharding import Mesh, PartitionSpec as P

coef = 0.7978845608
bf16 = jnp.bfloat16
f32 = jnp.float32
SWAP = [(0, 1), (1, 0)]
CROSS = [(0, 3), (1, 2), (2, 1), (3, 0)]
GRID = ("x", "y")
ROW4 = ("rm", "rl")


def gelu_pair(pre):
    inner = coef * (pre + 0.044715 * pre * pre * pre)
    tanh_v = jnp.tanh(inner)
    act = 0.5 * pre * (1.0 + tanh_v)
    slope = 0.5 * (1.0 + tanh_v) + 0.5 * pre * (1.0 - tanh_v * tanh_v) * coef * (
        1.0 + 0.134145 * pre * pre
    )
    return (act, slope)


def dot(left, right):
    return jnp.dot(left, right, preferred_element_type=f32)


def against(left, right):
    return lax.dot_general(left, right, (((1,), (1,)), ((), ())), preferred_element_type=f32)


def over_rows(left, right):
    return lax.dot_general(left, right, (((0,), (0,)), ((), ())), preferred_element_type=f32)


def part_of(whole, at, size, dim):
    return lax.dynamic_slice_in_dim(whole, at * size, size, dim)


def swap(value, axis):
    return lax.ppermute(value, axis, SWAP)


def join(mine, other, axis, dim):
    first = lax.axis_index(axis) == 0
    return jnp.where(
        first,
        jnp.concatenate([mine, other], dim),
        jnp.concatenate([other, mine], dim),
    )


def after(first, *values):
    kept = lax.optimization_barrier((first, *values))[1:]
    return kept[0] if len(kept) == 1 else kept


def cut(part, axis, dim):
    size = part.shape[dim] // 2
    at = lax.axis_index(axis)
    return part_of(part, at, size, dim), part_of(part, 1 - at, size, dim).astype(bf16)


def cross(value):
    return lax.ppermute(value, ("rh", "zh"), CROSS)


def spread(rows, axes):
    n = lax.axis_size(axes)
    sent = jnp.broadcast_to(rows[None], (n,) + rows.shape)
    got = lax.all_to_all(sent, axes, 0, 0, tiled=True)
    return got.reshape(n * rows.shape[0], rows.shape[1])


def deal(part, axes):
    n = lax.axis_size(axes)
    got = lax.all_to_all(part.reshape(n, -1, part.shape[1]), axes, 0, 0, tiled=True)
    total = got[0].astype(f32)
    for at in range(1, n):
        total = total + got[at].astype(f32)
    return total


def shards(tokens, cotangent, w_in, b_in, w_out):
    zh = lax.axis_index("zh")
    core = lax.axis_index("core")
    tok_dev, feat = tokens.shape
    quarter = w_in.shape[1]
    half_h = 2 * quarter
    quarter_d = w_out.shape[1]
    half_d = 2 * quarter_d

    kept = jnp.concatenate([tokens, part_of(cotangent, zh, half_d, 1)], 1)
    sent = jnp.concatenate([tokens, part_of(cotangent, 1 - zh, half_d, 1)], 1)
    got = swap(sent, "zh")
    rows = join(kept, got, "zh", 0)
    w_out = after(rows, w_out)
    out_pair = after(rows, join(w_out, swap(w_out, "core"), "core", 1))

    every_g = spread(rows[:, feat:], GRID)
    every_x = spread(after(every_g, rows[:, :feat]), GRID)

    back = against(every_g, out_pair).reshape(2, 2, -1, 2 * half_h)
    back_kept, back_sent = cut(back, "rl", 1)
    w_in = after(back_sent, w_in)
    in_pair = after(rows, join(w_in, swap(w_in, "core"), "core", 1))
    back_kept, back_sent = cut(back_kept + swap(back_sent, "rl").astype(f32), "rm", 0)
    every_x = after((back_sent, in_pair), every_x)
    pre = dot(every_x, in_pair).astype(bf16)
    back_got = swap(back_sent, "rm")
    pre = deal(after(back_got, pre), ROW4).astype(bf16)
    back_kept, back_sent = cut((back_kept + back_got.astype(f32))[0, 0], "zh", 1)
    back = (back_kept + cross(back_sent).astype(f32)).astype(bf16)
    pair_x = swap(every_x, "core")
    pair_g = swap(part_of(every_g, 1 - core, quarter_d, 1), "core")
    pre = after((pair_x, pair_g), pre)
    met = jnp.concatenate([pre, back], 1)
    met = met.astype(f32) + swap(met, "rh").astype(f32)
    pre, back = met[:, :half_h], met[:, half_h:]

    act_f, slope = gelu_pair(pre + part_of(b_in, zh, half_h, 0))
    act = act_f.astype(bf16)
    crossed = cross(act)
    grad = spread((back * slope).astype(bf16), ROW4)
    part = against(grad, in_pair).astype(bf16)
    dealt = lax.all_to_all(part.reshape(-1, 2 * tok_dev, feat), GRID, 0, 0, tiled=True)

    own_grad = part_of(grad, core, quarter, 1)
    act = join(act, after(part, crossed), "zh", 1)[None, None]
    act = join(act, swap(act, "rm"), "rm", 0)
    own_part = over_rows(every_x, after(act, own_grad))
    pair_grad = swap(after(own_part, part_of(grad, 1 - core, quarter, 1)), "core")
    act = join(act, after(dealt, swap(after(own_part, act), "rl")), "rl", 1).reshape(-1, act.shape[-1])
    w_in_grad = (own_part + over_rows(pair_x, pair_grad)).astype(bf16)
    b_in_grad = jnp.sum(own_grad.astype(f32), 0) + jnp.sum(pair_grad.astype(f32), 0)

    summed = jnp.sum(after((w_in_grad, b_in_grad), dealt).astype(f32), axis=0)
    out_rows = part_of(summed, 1 - zh, tok_dev, 0).astype(bf16)
    own_rows = part_of(summed, zh, tok_dev, 0)
    own_g = part_of(every_g, core, quarter_d, 1)
    pair_act = swap(after(out_rows, act), "core")
    w_out_grad = (over_rows(act, own_g) + over_rows(pair_act, pair_g)).astype(bf16)
    got_rows = after(w_out_grad, swap(out_rows, "zh"))
    input_grad = (own_rows + got_rows.astype(f32)).astype(bf16)
    return (input_grad, w_in_grad, b_in_grad, w_out_grad)


def solution(mesh):
    grid = Mesh(
        mesh.devices.reshape(2, 2, 2, 4, 4, 2, 2), ("rh", "rm", "rl", "x", "y", "zh", "core")
    )
    row, col, depth = ("rh", "rm", "rl"), ("x", "y"), ("zh", "core")
    return jax.shard_map(
        shards,
        mesh=grid,
        in_specs=(
            P(col + depth, row),
            P(col + depth, row),
            P(row, col + depth),
            P(col),
            P(col, row + depth),
        ),
        out_specs=(
            P(col + depth, row),
            P(row, col + depth),
            P(col + depth),
            P(col, row + depth),
        ),
        check_vma=False,
    )
```
